128 devices in a mesh: dp: 4 (over x), expert: 32 (over z, y, core).
Axes of the slice: x: 4, y: 4, z: 4, core: 2. Of those that a mesh axis runs over, the one named last changes fastest.
Arguments:
- tokens: bfloat16 [2048, 7168], P('expert', 'dp'), may hold values from -6 to 6
- cotangent: bfloat16 [2048, 7168], P('expert', 'dp'), may hold values from -6 to 6
- expert_ids: int32 [2048, 8], P('expert'), may hold values from 0 to 31, all different within a row; in each aligned block of 64 rows (0 to 63, 64 to 127, ...) at most 20 rows name the same one
- gate_values: float32 [2048, 8], P('expert'), may hold values from 0.05 to 1
- gate_up_weight: bfloat16 [32, 2, 7168, 1024], P('expert', None, None, 'dp'), may hold values from -0.0625 to 0.0625
- down_weight: bfloat16 [32, 1024, 7168], P('expert', 'dp'), may hold values from -0.1875 to 0.1875
Outputs:
- output: bfloat16 [2048, 7168], P('expert', 'dp')
- input_grad: bfloat16 [2048, 7168], P('expert', 'dp')
- grad_gate_up: bfloat16 [32, 2, 7168, 1024], P('expert', None, None, 'dp')
- grad_down: bfloat16 [32, 1024, 7168], P('expert', 'dp')
The draws below stay inside these ranges and needn't reach their ends.
Inputs may be any that keep to these rules, and one draw needn't show every extreme that they name: `expert_ids`: each row names 8 different experts. Within the rows of one device (aligned blocks of 64 rows) no expert is named by more than 20 rows, and in some block one expert is named by exactly 20 rows.
All inputs are finite; a program needn't handle non-finite values.
Results may differ from the reference program's by a relative error of at most 0.013.
Values may be sent and summed in bfloat16 or wider, within the bound.
No kernel may reach another device: no remote copies, remote signals or barrier semaphores. Data moves between devices by JAX's collectives and lax.ppermute only.
A program may use at most 192 MiB of HBM per device.

```python
import math
import jax
import jax.numpy as jnp
import numpy as np
from jax import lax

D = 7168
H = 1024
TOP = 8
TOKB = 64
EXPERTS = 32
CAP = 20
TOKENS = 2048
N_DP = 4


def shard_levels(rng, extent, pieces, least, top_value):
    gain = 1.0
    for dim, parts in pieces:
        draws = jax.random.uniform(jax.random.fold_in(jax.random.fold_in(rng, 6), dim), (parts,), jnp.float32, least / len(pieces), top_value / len(pieces))
        gain = gain * jnp.repeat(jnp.exp(draws), extent[dim] // parts).reshape((-1,) + (1,) * (len(extent) - 1 - dim))
    return gain


def shared_out(rng, own, number, rows, count, top, limit, skew):
    ranking = jax.random.permutation(rng, count)
    crowded, common = portions_of(count, rows * top, limit, skew, True), portions_of(count, rows * top, limit, skew, False)
    places = jnp.arange(count)

    def named(tallies, offset_by):
        used = int((tallies > 0).sum())
        fixed = max(1, used // 4)
        shifted = fixed + (places - fixed + offset_by * (used - fixed)) % max(1, count - fixed)
        return jnp.zeros((count,), jnp.int32).at[ranking[jnp.where(places < fixed, places, shifted)]].set(jnp.asarray(tallies, jnp.int32))

    tallies = jnp.where(number % 4 == 0, named(crowded, number // 4), named(common, number - number // 4 - 1))
    mixed = jax.random.permutation(jax.random.fold_in(own, 3), count)
    donor, taker = mixed[0:count // 2 * 2:2], mixed[1:count // 2 * 2:2]
    margin = jnp.minimum(tallies[donor] - 1, limit - tallies[taker]) // 2
    margin = jnp.where((donor == ranking[0]) | (taker == ranking[0]) | (tallies[taker] == 0), 0, jnp.maximum(margin, 0))
    shifted = jax.random.randint(jax.random.fold_in(own, 4), (count // 2,), 0, 1 << 20) % (margin + 1)
    tallies = tallies.at[donor].add(-shifted).at[taker].add(shifted)
    members = jnp.searchsorted(jnp.cumsum(tallies), jnp.arange(rows * top), side="right").astype(jnp.int32)
    grid = members.reshape(top, rows).T
    grid = grid[jax.random.permutation(jax.random.fold_in(own, 1), rows)]
    offset_by = jax.random.randint(jax.random.fold_in(own, 2), (rows, 1), 0, top)
    return jnp.take_along_axis(grid, (jnp.arange(top)[None, :] + offset_by) % top, axis=1)


def portions_of(amount, total, most, skew, full):
    loads = [(1 << 20) // math.isqrt(grade ** skew) + 1 for grade in range(1, amount + 1)]
    largest = most if full else min(most, max(-(-total // amount), total * loads[0] // sum(loads)))
    least = 1 if total - largest >= amount - 1 else 0
    given, spare = [largest] + [least] * (amount - 1), total - largest - least * (amount - 1)
    while spare > 0:
        movable = [i for i in range(1, amount) if given[i] < largest] or [i for i in range(1, amount) if given[i] < most]
        pool, remaining = sum([loads[i] for i in movable]), spare
        for i in movable:
            more = min(most - given[i], max(1, remaining * loads[i] // pool), spare)
            given[i] = given[i] + more
            spare = spare - more
    return np.array(given)


def bell_draw(rng, shape, scale, limit, pieces=(), kind=jnp.bfloat16):
    factor_of = shard_levels(rng, shape, pieces, -0.22, 0.18) if pieces else 1.0
    array = jax.random.normal(rng, shape, jnp.float32) * scale * factor_of
    return jnp.minimum(jnp.maximum(array, -limit), limit).astype(kind)


def setup_inputs(seed: int = 0) -> dict:
    seeds = jax.random.split(jax.random.key(seed), 7)
    tokens = bell_draw(seeds[0], (TOKENS, D), 1.0, 6.0, ((0, 32), (1, 4)))
    cotangent = bell_draw(seeds[1], (TOKENS, D), 1.0, 6.0, ((0, 32), (1, 4)))
    expert_ids_keys = jax.random.split(jax.random.fold_in(seeds[2], 1), TOKENS // TOKB)
    expert_ids_turns = jax.random.permutation(jax.random.fold_in(seeds[2], 3), TOKENS // TOKB)
    expert_ids = jax.vmap(lambda own, number: shared_out(jax.random.fold_in(seeds[2], 2), own, number, TOKB, EXPERTS, TOP, CAP, 2))(expert_ids_keys, expert_ids_turns).reshape((TOKENS, TOP))
    gate_values = jnp.clip(jnp.exp(math.log(1.0) - 2.9957323 * jax.random.uniform(seeds[3], (TOKENS, TOP), jnp.float32) ** shard_levels(seeds[3], (TOKENS, TOP), ((0, 32),), -0.2, 0.2)), 0.05, 1.0)
    gate_up_weight = bell_draw(seeds[4], (EXPERTS, 2, D, H), D ** -0.5, 0.0625, ((0, 32), (3, 4)))
    down_weight = bell_draw(seeds[5], (EXPERTS, H, D), H ** -0.5, 0.1875, ((0, 32), (1, 4)))
    return dict(tokens=tokens, cotangent=cotangent, expert_ids=expert_ids, gate_values=gate_values, gate_up_weight=gate_up_weight, down_weight=down_weight)


def reference(tokens, cotangent, expert_ids, gate_values, gate_up_weight, down_weight):
    token_count = TOKENS
    row_limit = EXPERTS * CAP
    group_width = H // N_DP

    def one_expert(running, inputs):
        out_acc, in_acc = running
        expert, gate_up_one, down_one = inputs
        chosen = expert_ids == expert
        weight = jnp.sum(jnp.where(chosen, gate_values, 0.0), axis=1)
        routed_here = jnp.any(chosen, axis=1)
        indices = jnp.arange(token_count, dtype=jnp.int32)
        sort_keys = jnp.where(routed_here, indices, indices + token_count)
        picked = jnp.argsort(sort_keys, stable=True)[:row_limit].astype(jnp.int32)
        live_rows = routed_here[picked]
        row_gate = jnp.where(live_rows, weight[picked], 0.0)
        rows_in = tokens[picked]
        gate_up_f = gate_up_one.astype(jnp.float32)
        down_f = down_one.astype(jnp.float32)
        pre = jnp.einsum("rd,cdh->rch", rows_in.astype(jnp.float32), gate_up_f)
        gate_pre = pre[:, 0]
        up_pre = pre[:, 1]
        sigmoid_gate = jax.nn.sigmoid(gate_pre)
        silu_gate = gate_pre * sigmoid_gate
        hidden = (silu_gate * up_pre).astype(jnp.bfloat16)
        hidden_groups = hidden.astype(jnp.float32).reshape(row_limit, N_DP, group_width)
        down_groups = down_f.reshape(N_DP, group_width, D)
        group_parts = jnp.einsum("rgh,ghd->grd", hidden_groups, down_groups).astype(jnp.bfloat16)
        out_rows = jnp.sum(group_parts.astype(jnp.float32), axis=0).astype(jnp.bfloat16)
        out_acc = out_acc.at[picked].add(row_gate[:, None] * out_rows.astype(jnp.float32))
        back = (row_gate[:, None] * cotangent[picked].astype(jnp.float32)).astype(jnp.bfloat16)
        back_f = back.astype(jnp.float32)
        grad_hidden = jnp.einsum("rd,hd->rh", back_f, down_f)
        grad_gate = (grad_hidden * up_pre * sigmoid_gate * (1.0 + gate_pre * (1.0 - sigmoid_gate))).astype(jnp.bfloat16)
        grad_up = (grad_hidden * silu_gate).astype(jnp.bfloat16)
        grad_pre = jnp.stack([grad_gate, grad_up], axis=1).astype(jnp.float32)
        grad_down_one = jnp.einsum("rh,rd->hd", hidden.astype(jnp.float32), back_f).astype(jnp.bfloat16)
        grad_gate_up_one = jnp.einsum("rd,rch->cdh", rows_in.astype(jnp.float32), grad_pre).astype(jnp.bfloat16)
        pre_groups = grad_pre.reshape(row_limit, 2, N_DP, group_width)
        weight_groups = gate_up_f.reshape(2, D, N_DP, group_width)
        in_parts = jnp.einsum("rcgh,cdgh->grd", pre_groups, weight_groups).astype(jnp.bfloat16)
        in_rows = jnp.sum(in_parts.astype(jnp.float32), axis=0).astype(jnp.bfloat16)
        in_acc = in_acc.at[picked].add(jnp.where(live_rows[:, None], in_rows.astype(jnp.float32), 0.0))
        return (out_acc, in_acc), (grad_gate_up_one, grad_down_one)

    start = (jnp.zeros((token_count, D), jnp.float32), jnp.zeros((token_count, D), jnp.float32))
    experts_list = jnp.arange(EXPERTS, dtype=jnp.int32)
    finals, grads = lax.scan(one_expert, start, (experts_list, gate_up_weight, down_weight))
    output = finals[0].astype(jnp.bfloat16)
    input_grad = finals[1].astype(jnp.bfloat16)
    return output, input_grad, grads[0], grads[1]
```

```python
import functools

import jax
import jax.numpy as jnp
from jax import lax
from jax.experimental import pallas as pl
from jax.experimental.pallas import tpu as pltpu
from jax.sharding import PartitionSpec as P

NX, NY, NZ, NC = 4, 4, 4, 2
BF16, F32 = jnp.bfloat16, jnp.float32
VMEM_LIMIT = 48 * 1024 * 1024


def expert_perm(dz, dy, flip):
    pairs = []
    for z in range(NZ):
        for y in range(NY):
            for c in range(NC):
                target = (((z + dz) % NZ) * NY + (y + dy) % NY) * NC + (c ^ flip)
                pairs.append(((z * NY + y) * NC + c, target))
    return pairs


def shift_z(v, d):
    return lax.ppermute(v, "expert", expert_perm(d, 0, 0))


def shift_y(v, d):
    return lax.ppermute(v, "expert", expert_perm(0, d, 0))


def swap_core(v):
    return lax.ppermute(v, "expert", expert_perm(0, 0, 1))


def shift_x(v, d):
    return lax.ppermute(v, "dp", [(i, (i + d) % NX) for i in range(NX)])


def params():
    return pltpu.CompilerParams(vmem_limit_bytes=VMEM_LIMIT)


def cost(flops, moved):
    return pl.CostEstimate(flops=int(flops), bytes_accessed=int(moved), transcendentals=0)


def tile_of(width):
    for t in (768, 640, 512, 384, 256, 128):
        if width % t == 0:
            return t


def tables(meta, cap):
    me = lax.axis_index("expert")
    z, rest = me // (NY * NC), me % (NY * NC)
    ids, gates = meta[:, :8], meta[:, 8:16]
    count = meta.shape[0]
    owners = (((z + jnp.arange(NZ, dtype=jnp.int32)) % NZ) * (NY * NC) + rest).astype(F32)
    same = ids[:, None, :] == owners[None, :, None]
    chosen = jnp.sum(same.astype(F32), axis=2)
    weight = jnp.sum(jnp.where(same, gates[:, None, :], 0.0), axis=2)
    below = (
        lax.broadcasted_iota(jnp.int32, (count, count), 0)
        > lax.broadcasted_iota(jnp.int32, (count, count), 1)
    ).astype(BF16)
    rank = jnp.dot(below, chosen.astype(BF16), preferred_element_type=F32)
    rank = jnp.where(chosen > 0, rank, -1.0)
    place = jnp.arange(cap, dtype=jnp.int32).astype(F32)
    hit = rank[:, :, None] == place[None, None, :]
    back = hit.astype(BF16).reshape(count, NZ * cap)
    full = jnp.where(hit, weight[:, :, None], 0.0).reshape(count, NZ * cap)
    high = lax.reduce_precision(full, 8, 7)
    low = (full - high).astype(BF16)
    rank_t, weight_t = rank.T, weight.T
    hit_t = rank_t[:, None, :] == place[None, :, None]
    pick = hit_t.astype(BF16).reshape(NZ * cap, count)
    slot_gate = jnp.sum(jnp.where(hit_t, weight_t[:, None, :], 0.0), axis=2).reshape(NZ * cap, 1)
    return pick, slot_gate, back, high.astype(BF16), low


def pick_kernel(gated, cap, *refs):
    pick_ref, rest = refs[0], refs[1:]
    if gated:
        gate_ref, rest = rest[0], rest[1:]
    own_ref, other_ref, outs = rest[0], rest[1], rest[2:]
    half = own_ref.shape[0]
    rows = jnp.dot(pick_ref[:, :half], own_ref[...], preferred_element_type=F32)
    rows += jnp.dot(pick_ref[:, half:], other_ref[...], preferred_element_type=F32)
    if gated:
        rows = rows * gate_ref[...]
    rows = rows.astype(BF16)
    for d in range(NZ):
        outs[d][...] = rows[d * cap : (d + 1) * cap]


def pick_rows(pick, own, other, gate=None):
    slots, count = pick.shape
    cap = slots // NZ
    half, width = own.shape
    t = tile_of(width)
    operands = [pick] + ([gate] if gate is not None else []) + [own, other]
    specs = [pl.BlockSpec((slots, count), lambda i: (0, 0))]
    if gate is not None:
        specs.append(pl.BlockSpec((slots, 1), lambda i: (0, 0)))
    specs += [pl.BlockSpec((half, t), lambda i: (0, i))] * 2
    return pl.pallas_call(
        functools.partial(pick_kernel, gate is not None, cap),
        grid=(width // t,),
        in_specs=specs,
        out_specs=[pl.BlockSpec((cap, t), lambda i: (0, i))] * NZ,
        out_shape=[jax.ShapeDtypeStruct((cap, width), BF16)] * NZ,
        compiler_params=params(),
        cost_estimate=cost(2 * slots * count * width, 2 * (slots + count) * width),
        name="pick_rows",
    )(*operands)


def combine_kernel(terms, *refs):
    tables_, pieces, outs = refs[:terms], refs[terms : terms + NZ], refs[terms + NZ :]
    rows = jnp.concatenate([p[...] for p in pieces], axis=0)
    total = jnp.dot(tables_[0][...], rows, preferred_element_type=F32)
    for table in tables_[1:]:
        total += jnp.dot(table[...], rows, preferred_element_type=F32)
    half = outs[0].shape[0]
    outs[0][...] = total[:half].astype(BF16)
    outs[1][...] = total[half:].astype(BF16)


def combine_rows(weights, pieces):
    count, slots = weights[0].shape
    cap, width = pieces[0].shape
    t = tile_of(width)
    half = count // 2
    return pl.pallas_call(
        functools.partial(combine_kernel, len(weights)),
        grid=(width // t,),
        in_specs=[pl.BlockSpec((count, slots), lambda i: (0, 0))] * len(weights)
        + [pl.BlockSpec((cap, t), lambda i: (0, i))] * NZ,
        out_specs=[pl.BlockSpec((half, t), lambda i: (0, i))] * 2,
        out_shape=[jax.ShapeDtypeStruct((half, width), BF16)] * 2,
        compiler_params=params(),
        cost_estimate=cost(
            2 * slots * count * width * len(weights), 2 * (slots + count) * width
        ),
        name="combine_rows",
    )(*weights, *pieces)


def call(kernel, me, grid, in_specs, out_specs, out_shape, operands, flops, moved, scratch=(), name=None):
    return pl.pallas_call(
        kernel,
        grid_spec=pltpu.PrefetchScalarGridSpec(
            num_scalar_prefetch=1,
            grid=grid,
            in_specs=in_specs,
            out_specs=out_specs,
            scratch_shapes=list(scratch),
        ),
        out_shape=out_shape,
        compiler_params=params(),
        cost_estimate=cost(flops, moved),
        name=name,
    )(me, *operands)


def place(j, me_ref):
    return (j - me_ref[0] + NX) % NX


NT = (((1,), (1,)), ((), ()))
TN = (((0,), (0,)), ((), ()))


def mm(a, b, dims=(((1,), (0,)), ((), ()))):
    return lax.dot_general(a, b, dims, preferred_element_type=F32)


def pre_b_kernel(fa, me_ref, x_ref, w_ref, pre_ref):
    @pl.when(pl.program_id(0) == 0)
    def _():
        pre_ref[...] = jnp.zeros_like(pre_ref)

    for c in range(2):
        pre_ref[c] += mm(x_ref[...], w_ref[c, fa:, :])


def pre_a_kernel(fa, me_ref, x_ref, w_ref, start_ref, hidden_ref, gate_ref, up_ref):
    @pl.when(pl.program_id(0) == 0)
    def _():
        gate_ref[...] = start_ref[0]
        up_ref[...] = start_ref[1]

    gate_ref[...] += mm(x_ref[0], w_ref[0, :fa, :])
    up_ref[...] += mm(x_ref[0], w_ref[1, :fa, :])

    @pl.when(pl.program_id(0) == NX - 1)
    def _():
        a = gate_ref[...]
        hidden_ref[...] = (a * jax.nn.sigmoid(a) * up_ref[...]).astype(BF16)


def out_kernel(fa, me_ref, h_ref, w_ref, oa_ref, ob_ref):
    oa_ref[0] = mm(h_ref[...], w_ref[:, :fa]).astype(BF16)
    ob_ref[...] = mm(h_ref[...], w_ref[:, fa:]).astype(BF16)


def gh_b_kernel(fa, me_ref, x_ref, w_ref, gh_ref):
    @pl.when(pl.program_id(0) == 0)
    def _():
        gh_ref[...] = jnp.zeros_like(gh_ref)

    gh_ref[...] += mm(x_ref[...], w_ref[:, fa:], NT)


def gh_a_kernel(fa, me_ref, x_ref, w_ref, start_ref, gate_ref, up_ref, gp_ref, acc):
    @pl.when(pl.program_id(0) == 0)
    def _():
        acc[...] = start_ref[...]

    acc[...] += mm(x_ref[0], w_ref[:, :fa], NT)

    @pl.when(pl.program_id(0) == NX - 1)
    def _():
        gh, a, b = acc[...], gate_ref[...], up_ref[...]
        s = jax.nn.sigmoid(a)
        gp_ref[0] = (gh * b * s * (1.0 + a * (1.0 - s))).astype(BF16)
        gp_ref[1] = (gh * (a * s)).astype(BF16)


def in_kernel(fa, me_ref, gp_ref, w_ref, oa_ref, ob_ref):
    oa_ref[0] = (mm(gp_ref[0], w_ref[0, :fa, :], NT) + mm(gp_ref[1], w_ref[1, :fa, :], NT)).astype(BF16)
    ob_ref[...] = (mm(gp_ref[0], w_ref[0, fa:, :], NT) + mm(gp_ref[1], w_ref[1, fa:, :], NT)).astype(BF16)


def gd_kernel(fa, me_ref, h_ref, xa_ref, xb_ref, o_ref):
    o_ref[:, :fa] = mm(h_ref[...], xa_ref[0], TN).astype(BF16)
    o_ref[:, fa:] = mm(h_ref[...], xb_ref[...], TN).astype(BF16)


def gg_kernel(fa, me_ref, gp_ref, xa_ref, xb_ref, o_ref):
    for c in range(2):
        o_ref[c, :fa, :] = mm(xa_ref[0], gp_ref[c], TN).astype(BF16)
        o_ref[c, fa:, :] = mm(xb_ref[...], gp_ref[c], TN).astype(BF16)


class Expert:
    def __init__(self, me, gate_up, down, rows, fa, fb):
        self.me, self.gate_up, self.down = me, gate_up, down
        self.rows, self.fa, self.fb = rows, fa, fb
        hid, model = down.shape
        self.hid, self.model, self.sl = hid, model, fa + fb
        self.spec_a = pl.BlockSpec((1, rows, fa), lambda j, m: (j, 0, 0))
        self.spec_b = pl.BlockSpec((rows, fb), lambda j, m: (0, place(j, m)))
        self.spec_gu = pl.BlockSpec((2, self.sl, hid), lambda j, m: (0, j, 0))
        self.spec_dn = pl.BlockSpec((hid, self.sl), lambda j, m: (0, j))
        self.spec_h = pl.BlockSpec((rows, hid), lambda j, m: (0, 0))
        self.spec_h2 = pl.BlockSpec((2, rows, hid), lambda j, m: (0, 0, 0))
        self.sds = jax.ShapeDtypeStruct

    def run(self, kernel, ins, outs, shapes, operands, width, scratch=(), name=None):
        flops = 2 * self.rows * self.hid * width
        return call(
            functools.partial(kernel, self.fa), self.me, (NX,), ins, outs, shapes, operands,
            flops, 2 * self.rows * width + 2 * self.hid * width, scratch, name,
        )

    def pre_b(self, xb):
        return self.run(
            pre_b_kernel, [self.spec_b, self.spec_gu], self.spec_h2,
            self.sds((2, self.rows, self.hid), F32), (xb, self.gate_up), 2 * NX * self.fb, name="pre_b",
        )

    def pre_a(self, xa, start):
        f = self.sds((self.rows, self.hid), F32)
        return self.run(
            pre_a_kernel, [self.spec_a, self.spec_gu, self.spec_h2], [self.spec_h] * 3,
            [self.sds((self.rows, self.hid), BF16), f, f], (xa, self.gate_up, start), 2 * NX * self.fa, name="pre_a",
        )

    def out(self, hidden):
        return self.run(
            out_kernel, [self.spec_h, self.spec_dn], [self.spec_a, self.spec_b],
            [self.sds((NX, self.rows, self.fa), BF16), self.sds((self.rows, NX * self.fb), BF16)],
            (hidden, self.down), self.model, name="out",
        )

    def gh_b(self, xb):
        return self.run(
            gh_b_kernel, [self.spec_b, self.spec_dn], self.spec_h,
            self.sds((self.rows, self.hid), F32), (xb, self.down), NX * self.fb, name="gh_b",
        )

    def gh_a(self, xa, start, a, b):
        return self.run(
            gh_a_kernel, [self.spec_a, self.spec_dn, self.spec_h, self.spec_h, self.spec_h], self.spec_h2,
            self.sds((2, self.rows, self.hid), BF16), (xa, self.down, start, a, b), NX * self.fa,
            [pltpu.VMEM((self.rows, self.hid), F32)], name="gh_a",
        )

    def inp(self, gp):
        return self.run(
            in_kernel, [self.spec_h2, self.spec_gu], [self.spec_a, self.spec_b],
            [self.sds((NX, self.rows, self.fa), BF16), self.sds((self.rows, NX * self.fb), BF16)],
            (gp, self.gate_up), 2 * self.model, name="inp",
        )

    def grad_down(self, hidden, xa, xb):
        return self.run(
            gd_kernel, [self.spec_h, self.spec_a, self.spec_b], self.spec_dn,
            self.sds((self.hid, self.model), BF16), (hidden, xa, xb), self.model, name="grad_down",
        )

    def grad_gate_up(self, gp, xa, xb):
        return self.run(
            gg_kernel, [self.spec_h2, self.spec_a, self.spec_b], self.spec_gu,
            self.sds((2, self.model, self.hid), BF16), (gp, xa, xb), 2 * self.model, name="grad_gate_up",
        )


def gather_y(v):
    return jnp.concatenate([v] + [shift_y(v, d) for d in range(1, NY)], axis=0)


def group(v):
    own = gather_y(v)
    return own, swap_core(own)


def exchange_z(pieces):
    return [pieces[0]] + [shift_z(pieces[d], d) for d in range(1, NZ)]


def return_z(rows):
    cap = rows.shape[0] // NZ
    return [rows[:cap]] + [shift_z(rows[d * cap : (d + 1) * cap], -d) for d in range(1, NZ)]


def total(parts):
    acc = parts[0].astype(F32)
    for p in parts[1:]:
        acc = acc + p.astype(F32)
    return acc.astype(BF16)


def scatter_y(own, other):
    mine = total([own, swap_core(other)])
    n = mine.shape[0] // NY
    return total([mine[:n]] + [shift_y(mine[d * n : (d + 1) * n], -d) for d in range(1, NY)])


def scatter_x(v):
    n = v.shape[1] // NX
    return total([v[:, :n]] + [shift_x(v[:, d * n : (d + 1) * n], d) for d in range(1, NX)])


def body(tokens, cotangent, expert_ids, gate_values, gate_up_weight, down_weight):
    token_rows, width = tokens.shape
    top = expert_ids.shape[1]
    capacity = min(token_rows, 5 * token_rows * top // (4 * NZ * NY * NC))
    cap = capacity * NY * NC
    rows = NZ * cap
    fb = 768
    fa = width - fb
    me_x = lax.axis_index("dp").astype(jnp.int32).reshape(1)
    ex = Expert(me_x, gate_up_weight[0], down_weight[0], rows, fa, fb)

    meta = jnp.concatenate([expert_ids.astype(F32), gate_values], axis=1)
    meta_own, meta_other = group(meta)

    tok_a = group(tokens[:, :fa])
    both_b = jnp.concatenate([tokens[:, fa:], cotangent[:, fa:]], axis=1)
    parts = [both_b] + [shift_x(both_b, -d) for d in range(1, NX)]
    tok_b = group(jnp.concatenate([p[:, :fb] for p in parts], axis=1))
    cot_all = group(
        jnp.concatenate([cotangent[:, :fa]] + [p[:, fb:] for p in parts], axis=1)
    )
    cot_a = [v[:, :fa] for v in cot_all]
    cot_b = [v[:, fa:] for v in cot_all]

    pick, slot_gate, back, high, low = tables(
        jnp.concatenate([meta_own, meta_other], axis=0), cap
    )

    tok_slots_a = jnp.concatenate(exchange_z(pick_rows(pick, *tok_a)), axis=0)
    xa = lax.all_gather(tok_slots_a, "dp", axis=0, tiled=False)
    xb = jnp.concatenate(exchange_z(pick_rows(pick, *tok_b)), axis=0)
    cot_slots_a = jnp.concatenate(exchange_z(pick_rows(pick, *cot_a, slot_gate)), axis=0)
    ga = lax.all_gather(cot_slots_a, "dp", axis=0, tiled=False)
    gb = jnp.concatenate(exchange_z(pick_rows(pick, *cot_b, slot_gate)), axis=0)

    pre_b = ex.pre_b(xb)
    hidden, a, b = ex.pre_a(xa, pre_b)
    out_a, out_b = ex.out(hidden)
    gh_b = ex.gh_b(gb)
    gp = ex.gh_a(ga, gh_b, a, b)
    in_a, in_b = ex.inp(gp)
    grad_down = ex.grad_down(hidden, ga, gb)
    grad_gate_up = ex.grad_gate_up(gp, xa, xb)

    def home(part_a, part_b, weights):
        sum_a = lax.psum_scatter(
            part_a.reshape(NX * rows, fa), "dp", scatter_dimension=0, tiled=True
        )
        res_b = scatter_x(scatter_y(*combine_rows(weights, return_z(part_b))))
        res_a = scatter_y(*combine_rows(weights, return_z(sum_a)))
        return jnp.concatenate([res_a, res_b], axis=1)

    output = home(out_a, out_b, (high, low))
    input_grad = home(in_a, in_b, (back,))
    return output, input_grad, grad_gate_up[None], grad_down[None]


def solution(mesh):
    return jax.shard_map(
        body,
        mesh=mesh,
        in_specs=(
            P("expert", "dp"),
            P("expert", "dp"),
            P("expert", None),
            P("expert", None),
            P("expert", None, None, "dp"),
            P("expert", "dp", None),
        ),
        out_specs=(
            P("expert", "dp"),
            P("expert", "dp"),
            P("expert", None, None, "dp"),
            P("expert", "dp", None),
        ),
        check_vma=False,
    )
```

```python
import functools
import math

import jax
import jax.numpy as jnp
from jax import lax
from jax.experimental import pallas as pl
from jax.experimental.pallas import tpu as pltpu
from jax.sharding import PartitionSpec as P


NX, NY, NZ, NC = 4, 4, 4, 2
BF16, F32 = jnp.bfloat16, jnp.float32


DP, EXPERT = "dp", "expert"


VMEM_LIMIT = 48 * 1024 * 1024


def expert_perm(dz, dy, flip):
    pairs = []
    for z in range(NZ):
        for y in range(NY):
            for c in range(NC):
                target = (((z + dz) % NZ) * NY + (y + dy) % NY) * NC + (c ^ flip)
                pairs.append(((z * NY + y) * NC + c, target))
    return pairs


def shift_z(v, d):
    return lax.ppermute(v, EXPERT, expert_perm(d, 0, 0))


def shift_y(v, d):
    return lax.ppermute(v, EXPERT, expert_perm(0, d, 0))


def swap_core(v):
    return lax.ppermute(v, EXPERT, expert_perm(0, 0, 1))


def shift_x(v, d):
    return lax.ppermute(v, DP, [(i, (i + d) % NX) for i in range(NX)])


def params():
    return pltpu.CompilerParams(vmem_limit_bytes=VMEM_LIMIT)


def cost(flops, moved):
    return pl.CostEstimate(flops=int(flops), bytes_accessed=int(moved), transcendentals=0)


def tile_of(width):
    for t in (1024, 896, 768, 640, 512, 384, 256, 128):
        if width % t == 0:
            return t


def places(expert_ids, experts):
    count = expert_ids.shape[0]
    same = expert_ids[:, :, None] == jnp.arange(experts, dtype=jnp.int32)
    named = jnp.any(same, axis=1)
    below = (
        lax.broadcasted_iota(jnp.int32, (count, count), 0)
        > lax.broadcasted_iota(jnp.int32, (count, count), 1)
    ).astype(BF16)
    earlier = jnp.dot(below, named.astype(BF16), preferred_element_type=F32)
    return jnp.sum(jnp.where(same, earlier[:, None, :], 0.0), axis=2)


def tables(meta, owners, capacity):
    meta = meta.astype(F32)
    ids, spots = meta[:, :8], meta[:, 8:16]
    gates = meta[:, 16:24] + meta[:, 24:32] + meta[:, 32:40]
    count = meta.shape[0]
    rows = 2 * 4 * capacity
    same = ids[:, None, :] == owners.astype(F32)[None, :, None]
    chosen = jnp.any(same, axis=2)
    weight = jnp.sum(jnp.where(same, gates[:, None, :], 0.0), axis=2)
    spot = jnp.sum(jnp.where(same, spots[:, None, :], 0.0), axis=2)
    token = jnp.arange(count, dtype=jnp.int32)
    per = count // 8
    base = (((token // per) % 4) * 2 + token // (4 * per)) * capacity
    row = jnp.where(chosen, spot + base.astype(F32)[:, None], -1.0)
    number = jnp.arange(rows, dtype=jnp.int32).astype(F32)
    spread = (
        lax.broadcasted_iota(jnp.int32, (4, 4 * rows), 1) // rows
        == lax.broadcasted_iota(jnp.int32, (4, 4 * rows), 0)
    ).astype(F32)
    wanted = (jnp.arange(4 * rows, dtype=jnp.int32) % rows).astype(F32)
    hit = jnp.dot(row, spread, precision=lax.Precision.HIGHEST) == wanted[None, :]
    full = jnp.dot(weight, spread, precision=lax.Precision.HIGHEST)
    full = jnp.where(hit, full, 0.0)
    back = hit.astype(BF16)
    high = lax.reduce_precision(full, 8, 7)
    low = (full - high).astype(BF16)
    high = high.astype(BF16)
    row_t, weight_t = row.T, weight.T
    hit_t = row_t[:, None, :] == number[None, :, None]
    pick = hit_t.astype(BF16).reshape(4 * rows, count)
    slot_gate = jnp.sum(jnp.where(hit_t, weight_t[:, None, :], 0.0), axis=2).reshape(4 * rows, 1)
    return pick, slot_gate, back, high, low


def routes(expert_ids, gate_values, experts):
    first = lax.reduce_precision(gate_values, 8, 7)
    rest = gate_values - first
    second = lax.reduce_precision(rest, 8, 7)
    third = rest - second
    ids = expert_ids.astype(F32)
    columns = [ids, places(expert_ids, experts), first, second, third]
    packed = jnp.concatenate(columns, axis=1).astype(BF16)
    return jnp.pad(packed, ((0, 0), (0, 128 - packed.shape[1])))


def pick_kernel(gated, cap, *refs):
    pick_ref, rest = refs[0], refs[1:]
    if gated:
        gate_ref, rest = rest[0], rest[1:]
    own_ref, other_ref, outs = rest[0], rest[1], rest[2:]
    half = own_ref.shape[0]
    rows = jnp.dot(pick_ref[:, :half], own_ref[...], preferred_element_type=F32)
    rows += jnp.dot(pick_ref[:, half:], other_ref[...], preferred_element_type=F32)
    if gated:
        rows = rows * gate_ref[...]
    rows = rows.astype(BF16)
    for d in range(NZ):
        outs[d][...] = rows[d * cap : (d + 1) * cap]


def pick_rows(pick, own, other, width, start, gate=None):
    slots, count = pick.shape
    cap = slots // NZ
    half = own.shape[0]
    t = tile_of(math.gcd(width, start) if start else width)
    first = start // t
    operands = [pick] + ([gate] if gate is not None else []) + [own, other]
    specs = [pl.BlockSpec((slots, count), lambda i: (0, 0))]
    if gate is not None:
        specs.append(pl.BlockSpec((slots, 1), lambda i: (0, 0)))
    specs += [pl.BlockSpec((half, t), lambda i: (0, i + first))] * 2
    return pl.pallas_call(
        functools.partial(pick_kernel, gate is not None, cap),
        grid=(width // t,),
        in_specs=specs,
        out_specs=[pl.BlockSpec((cap, t), lambda i: (0, i))] * NZ,
        out_shape=[jax.ShapeDtypeStruct((cap, width), BF16)] * NZ,
        compiler_params=params(),
        cost_estimate=cost(2 * slots * count * width, 2 * (slots + count) * width),
    )(*operands)


def combine_kernel(terms, *refs):
    tables_, pieces, outs = refs[:terms], refs[terms : terms + NZ], refs[terms + NZ :]
    rows = jnp.concatenate([p[...] for p in pieces], axis=0)
    total = jnp.dot(tables_[0][...], rows, preferred_element_type=F32)
    for table in tables_[1:]:
        total += jnp.dot(table[...], rows, preferred_element_type=F32)
    half = outs[0].shape[0]
    outs[0][...] = total[:half].astype(BF16)
    outs[1][...] = total[half:].astype(BF16)


def combine_rows(weights, pieces):
    count, slots = weights[0].shape
    cap, width = pieces[0].shape
    t = tile_of(width)
    half = count // 2
    return pl.pallas_call(
        functools.partial(combine_kernel, len(weights)),
        grid=(width // t,),
        in_specs=[pl.BlockSpec((count, slots), lambda i: (0, 0))] * len(weights)
        + [pl.BlockSpec((cap, t), lambda i: (0, i))] * NZ,
        out_specs=[pl.BlockSpec((half, t), lambda i: (0, i))] * 2,
        out_shape=[jax.ShapeDtypeStruct((half, width), BF16)] * 2,
        compiler_params=params(),
        cost_estimate=cost(
            2 * slots * count * width * len(weights), 2 * (slots + count) * width
        ),
    )(*weights, *pieces)


def stack_kernel(*refs):
    n = refs[0].shape[0]
    for d in range(4):
        refs[4][d * n : (d + 1) * n, :] = refs[d][...]


def stack(pieces):
    n, width = pieces[0].shape
    t = tile_of(width)
    return pl.pallas_call(
        stack_kernel,
        grid=(width // t,),
        in_specs=[pl.BlockSpec((n, t), lambda i: (0, i))] * 4,
        out_specs=pl.BlockSpec((4 * n, t), lambda i: (0, i)),
        out_shape=jax.ShapeDtypeStruct((4 * n, width), BF16),
        compiler_params=params(),
        cost_estimate=cost(0, 16 * n * width),
    )(*pieces)


def call(kernel, me, grid, in_specs, out_specs, out_shape, operands, flops, moved, scratch=()):
    return pl.pallas_call(
        kernel,
        grid_spec=pltpu.PrefetchScalarGridSpec(
            num_scalar_prefetch=1,
            grid=grid,
            in_specs=in_specs,
            out_specs=out_specs,
            scratch_shapes=list(scratch),
        ),
        out_shape=out_shape,
        compiler_params=params(),
        cost_estimate=cost(flops, moved),
    )(me, *operands)


def place(j, me_ref):
    return (j - me_ref[0] + NX) % NX


NT = (((1,), (1,)), ((), ()))
TN = (((0,), (0,)), ((), ()))


def mm(a, b, dims=(((1,), (0,)), ((), ()))):
    return lax.dot_general(a, b, dims, preferred_element_type=F32)


def pre_b_kernel(fa, me_ref, x0, x1, x2, x3, w_ref, pre_ref):
    @pl.when(pl.program_id(0) == 0)
    def _():
        pre_ref[...] = jnp.zeros_like(pre_ref)

    for d, x_ref in enumerate((x0, x1, x2, x3)):
        n = x_ref.shape[0]
        for c in range(2):
            pre_ref[c, d * n : (d + 1) * n, :] += mm(x_ref[...], w_ref[c, fa:, :])


def pre_a_kernel(fa, me_ref, x_ref, w_ref, start_ref, hidden_ref, gate_ref, up_ref):
    @pl.when(pl.program_id(0) == 0)
    def _():
        gate_ref[...] = start_ref[0]
        up_ref[...] = start_ref[1]

    gate_ref[...] += mm(x_ref[0], w_ref[0, :fa, :])
    up_ref[...] += mm(x_ref[0], w_ref[1, :fa, :])

    @pl.when(pl.program_id(0) == NX - 1)
    def _():
        a = gate_ref[...]
        hidden_ref[...] = (a * jax.nn.sigmoid(a) * up_ref[...]).astype(BF16)


def out_kernel(fa, me_ref, h_ref, w_ref, oa_ref, *ob_refs):
    oa_ref[0] = mm(h_ref[...], w_ref[:, :fa]).astype(BF16)
    part = mm(h_ref[...], w_ref[:, fa:]).astype(BF16)
    for d, ob_ref in enumerate(ob_refs):
        n = ob_ref.shape[0]
        ob_ref[...] = part[d * n : (d + 1) * n]


def gh_b_kernel(fa, me_ref, x0, x1, x2, x3, w_ref, gh_ref):
    @pl.when(pl.program_id(0) == 0)
    def _():
        gh_ref[...] = jnp.zeros_like(gh_ref)

    for d, x_ref in enumerate((x0, x1, x2, x3)):
        n = x_ref.shape[0]
        q = n // 4
        part = mm(x_ref[...], w_ref[:, fa:], NT)
        for e in range(4):
            first = e * n + d * q
            gh_ref[first : first + q, :] += part[e * q : (e + 1) * q]


def gh_a_kernel(fa, me_ref, x_ref, w_ref, start_ref, gate_ref, up_ref, gp_ref, acc):
    @pl.when(pl.program_id(0) == 0)
    def _():
        acc[...] = start_ref[...]

    acc[...] += mm(x_ref[0], w_ref[:, :fa], NT)

    @pl.when(pl.program_id(0) == NX - 1)
    def _():
        gh, a, b = acc[...], gate_ref[...], up_ref[...]
        s = jax.nn.sigmoid(a)
        gp_ref[0] = (gh * b * s * (1.0 + a * (1.0 - s))).astype(BF16)
        gp_ref[1] = (gh * (a * s)).astype(BF16)


def in_a_kernel(fa, me_ref, gp_ref, w_ref, oa_ref):
    oa_ref[0] = (mm(gp_ref[0], w_ref[0], NT) + mm(gp_ref[1], w_ref[1], NT)).astype(BF16)


def in_b_kernel(fa, me_ref, gp_ref, w_ref, *ob_refs):
    part = mm(gp_ref[0], w_ref[0], NT) + mm(gp_ref[1], w_ref[1], NT)
    n = ob_refs[0].shape[0]
    q = n // 4
    for e in range(4):
        for d, ob_ref in enumerate(ob_refs):
            first = e * n + d * q
            ob_ref[e * q : (e + 1) * q, :] = part[first : first + q].astype(BF16)


def gd_kernel(fa, me_ref, h_ref, xa_ref, xb_ref, o_ref):
    o_ref[:, :fa] = mm(h_ref[...], xa_ref[0], TN).astype(BF16)
    o_ref[:, fa:] = mm(h_ref[...], xb_ref[...], TN).astype(BF16)


def gg_kernel(fa, me_ref, gp_ref, xa_ref, x0, x1, x2, x3, o_ref):
    x = jnp.concatenate([x_ref[...] for x_ref in (x0, x1, x2, x3)], axis=0)
    for c in range(2):
        o_ref[c, :fa, :] = mm(xa_ref[0], gp_ref[c], TN).astype(BF16)
        o_ref[c, fa:, :] = mm(x, gp_ref[c], TN).astype(BF16)


class Expert:
    def __init__(self, me, gate_up, down, rows, fb):
        self.me, self.gate_up, self.down = me, gate_up, down
        hid, model = down.shape
        self.hid, self.model, self.sl = hid, model, model // NX
        fa = self.sl - fb
        self.rows, self.fa, self.fb = rows, fa, fb
        self.spec_a = pl.BlockSpec((1, rows, fa), lambda j, m: (j, 0, 0))
        self.spec_b = pl.BlockSpec((rows, fb), lambda j, m: (0, place(j, m)))
        self.spec_p = [pl.BlockSpec((rows // 4, fb), lambda j, m: (0, place(j, m)))] * 4
        self.spec_gu = pl.BlockSpec((2, self.sl, hid), lambda j, m: (0, j, 0))
        self.spec_dn = pl.BlockSpec((hid, self.sl), lambda j, m: (0, j))
        self.spec_h = pl.BlockSpec((rows, hid), lambda j, m: (0, 0))
        self.spec_h2 = pl.BlockSpec((2, rows, hid), lambda j, m: (0, 0, 0))
        self.sds = jax.ShapeDtypeStruct

    def run(self, kernel, ins, outs, shapes, operands, width, scratch=()):
        flops = 2 * self.rows * self.hid * width
        return call(
            functools.partial(kernel, self.fa), self.me, (NX,), ins, outs, shapes, operands,
            flops, 2 * self.rows * width + 2 * self.hid * width, scratch,
        )

    def pre_b(self, xb):
        return self.run(
            pre_b_kernel, [*self.spec_p, self.spec_gu], self.spec_h2,
            self.sds((2, self.rows, self.hid), F32), (*xb, self.gate_up), 2 * NX * self.fb,
        )

    def pre_a(self, xa, start):
        f = self.sds((self.rows, self.hid), F32)
        return self.run(
            pre_a_kernel, [self.spec_a, self.spec_gu, self.spec_h2], [self.spec_h] * 3,
            [self.sds((self.rows, self.hid), BF16), f, f], (xa, self.gate_up, start), 2 * NX * self.fa,
        )

    def out(self, hidden):
        return self.run(
            out_kernel, [self.spec_h, self.spec_dn], [self.spec_a, *self.spec_p],
            [self.sds((NX, self.rows, self.fa), BF16)] + [self.sds((self.rows // 4, NX * self.fb), BF16)] * 4,
            (hidden, self.down), self.model,
        )

    def gh_b(self, xb):
        return self.run(
            gh_b_kernel, [*self.spec_p, self.spec_dn], self.spec_h,
            self.sds((self.rows, self.hid), F32), (*xb, self.down), NX * self.fb,
        )

    def gh_a(self, xa, start, a, b):
        return self.run(
            gh_a_kernel, [self.spec_a, self.spec_dn, self.spec_h, self.spec_h, self.spec_h], self.spec_h2,
            self.sds((2, self.rows, self.hid), BF16), (xa, self.down, start, a, b), NX * self.fa,
            [pltpu.VMEM((self.rows, self.hid), F32)],
        )

    def half(self, which):
        assert self.fa == self.fb
        return pl.BlockSpec((2, self.fa, self.hid), lambda j, m: (0, 2 * j + which, 0))

    def in_a(self, gp):
        return self.run(
            in_a_kernel, [self.spec_h2, self.half(0)], self.spec_a,
            self.sds((NX, self.rows, self.fa), BF16), (gp, self.gate_up), 2 * NX * self.fa,
        )

    def in_b(self, gp):
        return self.run(
            in_b_kernel, [self.spec_h2, self.half(1)], self.spec_p,
            [self.sds((self.rows // 4, NX * self.fb), BF16)] * 4, (gp, self.gate_up), 2 * NX * self.fb,
        )

    def grad_down(self, hidden, xa, xb):
        return self.run(
            gd_kernel, [self.spec_h, self.spec_a, self.spec_b], self.spec_dn,
            self.sds((self.hid, self.model), BF16), (hidden, xa, xb), self.model,
        )

    def grad_gate_up(self, gp, xa, xb):
        return self.run(
            gg_kernel, [self.spec_h2, self.spec_a, *self.spec_p], self.spec_gu,
            self.sds((2, self.model, self.hid), BF16), (gp, xa, *xb), 2 * self.model,
        )


def group(v, shift):
    moved = [shift(v, d) for d in range(1, 4)]
    if v.shape[1] > 2048:
        own = stack([v] + moved)
    else:
        own = jnp.concatenate([v] + moved, axis=0)
    return own, swap_core(own)


def exchange(pieces, shift):
    moved = [shift(pieces[d], d) for d in range(1, 4)]
    return [pieces[0]] + moved


def give_back(pieces, shift):
    moved = [shift(pieces[d], -d) for d in range(1, 4)]
    return [pieces[0]] + moved


def join_z(pieces):
    return jnp.concatenate(pieces, axis=0)


def cut_z(rows):
    n = rows.shape[0] // 4
    return [rows[d * n : (d + 1) * n] for d in range(4)]


def join_y(pieces):
    n, width = pieces[0].shape
    blocks = [p.reshape(NZ, 1, n // NZ, width) for p in pieces]
    return jnp.concatenate(blocks, axis=1).reshape(4 * n, width)


def cut_y(rows):
    n, width = rows.shape
    blocks = rows.reshape(NZ, NY, n // 16, width)
    return [blocks[:, d].reshape(n // 4, width) for d in range(4)]


def total(parts):
    acc = parts[0].astype(F32)
    for p in parts[1:]:
        acc = acc + p.astype(F32)
    return acc.astype(BF16)


def scatter(own, other, shift):
    came = swap_core(other)
    mine = total([own, came])
    n = mine.shape[0] // 4
    moved = [shift(mine[d * n : (d + 1) * n], -d) for d in range(1, 4)]
    return total([mine[:n]] + moved)


def body(tokens, cotangent, expert_ids, gate_values, gate_up_weight, down_weight):
    token_rows, _ = tokens.shape
    top = expert_ids.shape[1]
    experts = NZ * NY * NC
    capacity = min(token_rows, 5 * token_rows * top // (4 * experts))
    rows = experts * capacity
    me_x = lax.axis_index(DP).astype(jnp.int32).reshape(1)
    me = lax.axis_index(EXPERT)
    z, y, c = me // (NY * NC), (me // NC) % NY, me % NC
    away = jnp.arange(4, dtype=jnp.int32)
    owners_z = ((z + away) % NZ * NY + y) * NC + c
    owners_y = (z * NY + (y + away) % NY) * NC + c
    ex_t, ex_c, ex_o, ex_i = [
        Expert(me_x, gate_up_weight[0], down_weight[0], rows, fb) for fb in SPLITS
    ]
    fa_t, fa_c = ex_t.fa, ex_c.fa

    meta = routes(expert_ids, gate_values, experts)
    tok_a = group(jnp.concatenate([tokens[:, :fa_t], meta], axis=1), shift_y)
    both_b = jnp.concatenate([tokens[:, fa_t:], cotangent[:, fa_c:]], axis=1)
    parts = [both_b] + [shift_x(both_b, -d) for d in range(1, NX)]
    tok_b = group(jnp.concatenate([p[:, : ex_t.fb] for p in parts], axis=1), shift_y)

    meta_y = jnp.concatenate([v[:, fa_t:] for v in tok_a], axis=0)
    pick_t, _, _, high, low = tables(meta_y, owners_z, capacity)
    picked = pick_rows(pick_t, *tok_a, fa_t, 0)
    tok_slots_a = join_z(exchange(picked, shift_z))
    xa = lax.all_gather(tok_slots_a, DP, axis=0, tiled=False)

    meta, _ = lax.optimization_barrier((meta, picked[0]))
    cot_a = group(jnp.concatenate([cotangent[:, :fa_c], meta], axis=1), shift_z)
    cot_b = group(jnp.concatenate([p[:, ex_t.fb :] for p in parts], axis=1), shift_z)
    meta_z = jnp.concatenate([v[:, fa_c:] for v in cot_a], axis=0)
    pick_c, gate_c, back, _, _ = tables(meta_z, owners_y, capacity)

    picked = pick_rows(pick_c, *cot_a, fa_c, 0, gate_c)
    cot_slots_a = join_y(exchange(picked, shift_y))
    ga = lax.all_gather(cot_slots_a, DP, axis=0, tiled=False)
    picked = pick_rows(pick_t, *tok_b, NX * ex_t.fb, 0)
    xb = exchange(picked, shift_z)
    picked = pick_rows(pick_c, *cot_b, NX * ex_c.fb, 0, gate_c)
    gb = exchange(picked, shift_y)

    xb[0], back, high, low = lax.optimization_barrier((xb[0], back, high, low))
    pre_b = ex_t.pre_b(xb)
    hidden, a, b = ex_t.pre_a(xa, pre_b)
    out_a, *out_b = ex_o.out(hidden)
    gh_b = ex_c.gh_b(gb)
    gp = ex_c.gh_a(ga, gh_b, a, b)
    in_b = ex_i.in_b(gp)
    in_a = ex_i.in_a(gp)
    *gb, _ = lax.optimization_barrier((*gb, in_b[0]))
    grad_down = ex_c.grad_down(hidden, ga, join_y(gb))
    grad_gate_up = ex_t.grad_gate_up(gp, xa, xb)

    def sum_x(part):
        return lax.psum_scatter(
            part.reshape(NX * rows, part.shape[2]), DP, scatter_dimension=0, tiled=True
        )

    def combine(pieces, weights):
        return combine_rows(weights, pieces)

    out_sum, in_sum = sum_x(out_a), sum_x(in_a)
    halves_b = combine(give_back(out_b, shift_z), (high, low))
    halves_a = combine(give_back(cut_z(out_sum), shift_z), (high, low))
    outb_home = scatter(*halves_b, shift_y)
    outa_home = scatter(*halves_a, shift_y)
    halves_b = combine(give_back(in_b, shift_y), (back,))
    inb_home = scatter(*halves_b, shift_z)
    halves_a = combine(give_back(cut_y(in_sum), shift_y), (back,))
    ina_home = scatter(*halves_a, shift_z)

    fo, fi = ex_o.fb, ex_i.fb
    chunks = [
        jnp.concatenate(
            [
                outb_home[:, d * fo : (d + 1) * fo],
                inb_home[:, d * fi : (d + 1) * fi],
            ],
            axis=1,
        )
        for d in range(NX)
    ]
    moved = [shift_x(chunks[d], d) for d in range(1, NX)]
    both = total([chunks[0]] + moved)
    output = jnp.concatenate([outa_home, both[:, :fo]], axis=1)
    input_grad = jnp.concatenate([ina_home, both[:, fo:]], axis=1)
    return output, input_grad, grad_gate_up[None], grad_down[None]


SPLITS = (768, 896, 896, 896)


def solution(mesh):
    return jax.shard_map(
        body,
        mesh=mesh,
        in_specs=(
            P(EXPERT, DP),
            P(EXPERT, DP),
            P(EXPERT, None),
            P(EXPERT, None),
            P(EXPERT, None, None, DP),
            P(EXPERT, DP, None),
        ),
        out_specs=(
            P(EXPERT, DP),
            P(EXPERT, DP),
            P(EXPERT, None, None, DP),
            P(EXPERT, DP, None),
        ),
        check_vma=False,
    )
```
